32 devices in a mesh: ctx: 16 (over z, x, core), head: 2 (over y).
Axes of the slice: x: 2, y: 2, z: 4, core: 2. Of those that a mesh axis runs over, the one named last changes fastest.
Arguments:
- features: float32 [4096, 8192], P(('ctx', 'head')), may hold values from -200 to 200
- state_write: float32 [4096, 1024], P(('ctx', 'head')), may hold values from -6 to 6
- state_read: float32 [4096, 1024], P(('ctx', 'head')), may hold values from -6 to 6
- log_decay: float32 [4096, 128], P(('ctx', 'head')), may hold values from -0.6932 to 0, as said below
- conv_features: float32 [4, 8192], replicated, may hold values from -3 to 3
- conv_write: float32 [4, 1024], replicated, may hold values from -3 to 3
- conv_read: float32 [4, 1024], replicated, may hold values from -3 to 3
- norm_gain: float32 [8192], P('head'), may hold values from 0.5 to 1.5
Outputs:
- normed_head_outputs: float32 [4096, 8192], P('ctx', 'head')
The draws below stay inside these ranges and needn't reach their ends.
Inputs may be any that keep to these rules, and one draw needn't show every extreme that they name: `log_decay`: strictly negative.
All inputs are finite; a program needn't handle non-finite values.
Results may differ from the reference program's by a relative error of at most 0.00029.
Values sent between devices are 32-bit elements; how exact they have to be, the bound alone decides.
A program may use at most 128 MiB of HBM per device.

```python
import math
import jax
import jax.numpy as jnp
from jax import lax

H = 128
P_SIZE = 64
N = 128
G = 8
K = 4
L_DEV = 256
BLOCK = 256
SEQUENCE_LENGTH = 4096


def draw_features(key, part):
    first, second, third = jax.random.split(key, 3)
    base = jnp.clip(jax.random.normal(first, (SEQUENCE_LENGTH, H * P_SIZE), jnp.float32), -6.0, 6.0)
    rowwise = jnp.exp(jax.random.uniform(second, (SEQUENCE_LENGTH, 1), jnp.float32, 0.0, math.log(10.0)))
    colwise = jnp.exp(jax.random.uniform(third, (1, H * P_SIZE), jnp.float32, 0.0, math.log(10.0)))
    return base * rowwise * colwise / 3.0


def draw_log_decay(key, part):
    keys = jax.random.split(key, 7)
    share = 0.5
    rough_low = 0.5
    coarse_upper = 1.5
    slowly = jax.random.uniform(keys[0], (1, H), jnp.float32) < share
    slow_rate = jnp.exp(jax.random.uniform(keys[1], (1, H), jnp.float32, math.log(0.1), math.log(0.6))) / SEQUENCE_LENGTH
    fast_rate = jnp.exp(jax.random.uniform(keys[2], (1, H), jnp.float32, math.log(1.0 / 50.0), math.log(1.0 / 30.0)))
    rate = jnp.where(slowly, slow_rate, fast_rate)
    segment = jnp.exp(jax.random.uniform(keys[3], (SEQUENCE_LENGTH // L_DEV, H), jnp.float32, -math.log(2.0), math.log(2.0)))
    rough = jax.random.uniform(keys[4], (SEQUENCE_LENGTH, H), jnp.float32, rough_low, coarse_upper)
    payload_lines = -(rate * jnp.repeat(segment, L_DEV, 0) * rough)
    place_indices = jax.random.randint(keys[5], (2,), 0, SEQUENCE_LENGTH)
    span_cluster = jnp.any(jnp.arange(SEQUENCE_LENGTH)[:, None] == place_indices[None, :], 1)
    discarded_items = jnp.log(jax.random.uniform(keys[6], (SEQUENCE_LENGTH, H), jnp.float32, 0.55, 0.8))
    return jnp.where(span_cluster[:, None], discarded_items, payload_lines)


def shard_levels(key, shape, shards, smallest, largest):
    level, own = 1.0, jax.random.fold_in(key, 6)
    for axis_at, shards_of in shards:
        heights = jnp.exp(jax.random.uniform(jax.random.fold_in(own, axis_at), (shards_of,), jnp.float32, smallest / len(shards), largest / len(shards)))
        level = level * jnp.repeat(heights, shape[axis_at] // shards_of).reshape([-1 if axis == axis_at else 1 for axis in range(len(shape))])
    return level


def centred(rng, shape, width, bound, shards=(), held_as=jnp.bfloat16):
    drawn = width * jax.random.normal(rng, shape, jnp.float32)
    if shards:
        drawn = drawn * shard_levels(rng, shape, shards, -0.22, 0.18)
    return jnp.clip(drawn, -bound, bound).astype(held_as)


def setup_inputs(seed: int = 0) -> dict:
    seeds = jax.random.split(jax.random.key(seed), 9)
    return {
        "features": draw_features(jax.random.fold_in(seeds[8], 71), 0),
        "state_write": centred(seeds[1], (SEQUENCE_LENGTH, G * N), 1.0, 6.0, ((0, 32),), jnp.float32),
        "state_read": centred(seeds[2], (SEQUENCE_LENGTH, G * N), 1.0, 6.0, ((0, 32),), jnp.float32),
        "log_decay": draw_log_decay(jax.random.fold_in(seeds[8], 71), 0),
        "conv_features": centred(seeds[4], (K, H * P_SIZE), K ** -0.5, 3.0, (), jnp.float32),
        "conv_write": centred(seeds[5], (K, G * N), K ** -0.5, 3.0, (), jnp.float32),
        "conv_read": centred(seeds[6], (K, G * N), K ** -0.5, 3.0, (), jnp.float32),
        "norm_gain": jnp.clip(1.0 + 0.1 * jax.random.normal(seeds[7], (H * P_SIZE,), jnp.float32), 0.5, 1.5),
    }


highest = lax.Precision.HIGHEST
eps_norm = 1e-05

def causal_conv(tokens, leading, weight):
    tap_count = weight.shape[0]
    padded = jnp.concatenate([leading, tokens], 0)
    extent = tokens.shape[0]
    summed = weight[0] * padded[0:extent]
    for displacement in range(1, tap_count):
        summed = summed + weight[displacement] * padded[displacement:displacement + extent]
    return jax.nn.silu(summed)

def block_pass(carried_state, blocked):
    inputs_act, writes_act, reads_act, decays = blocked
    cumulative = jnp.cumsum(decays, 0)
    extent = decays.shape[0]
    target = lax.broadcasted_iota(jnp.int32, (extent, extent), 0)
    source = lax.broadcasted_iota(jnp.int32, (extent, extent), 1)
    strictly_past = target >= source
    along = jnp.transpose(cumulative, (1, 2, 0))
    spacing = jnp.where(strictly_past, along[..., :, None] - along[..., None, :], 0.0)
    damping = jnp.where(strictly_past, jnp.exp(spacing), 0.0)
    scores = jnp.einsum('tgn,sgn->gts', reads_act, writes_act, precision=highest)
    within_range = jnp.einsum('ghts,sghp->tghp', scores[:, None] * damping, inputs_act, precision=highest)
    entering = jnp.einsum('tgn,ghpn->tghp', reads_act, carried_state, precision=highest) * jnp.exp(cumulative)[..., None]
    remaining = jnp.exp(cumulative[-1] - cumulative)
    new_state = jnp.exp(cumulative[-1])[..., None, None] * carried_state + jnp.einsum('sgh,sghp,sgn->ghpn', remaining, inputs_act, writes_act, precision=highest)
    return (new_state, within_range + entering)

def reference(features, state_write, state_read, log_decay, conv_features, conv_write, conv_read, norm_gain):
    length = features.shape[0]
    tap_count = conv_features.shape[0]
    inputs_act = causal_conv(features, jnp.zeros((tap_count - 1, features.shape[1]), jnp.float32), conv_features)
    writes_act = causal_conv(state_write, jnp.zeros((tap_count - 1, state_write.shape[1]), jnp.float32), conv_write)
    reads_act = causal_conv(state_read, jnp.zeros((tap_count - 1, state_read.shape[1]), jnp.float32), conv_read)
    per_group = H // G
    blocks = length // BLOCK
    blocked = (inputs_act.reshape(blocks, BLOCK, G, per_group, P_SIZE), writes_act.reshape(blocks, BLOCK, G, N), reads_act.reshape(blocks, BLOCK, G, N), log_decay.reshape(blocks, BLOCK, G, per_group))
    initial = jnp.zeros((G, per_group, P_SIZE, N), jnp.float32)
    final_state, partial_value = lax.scan(block_pass, initial, blocked)
    mixed = partial_value.reshape(length, G, per_group * P_SIZE)
    inverse = lax.rsqrt(lax.optimization_barrier(jnp.mean(mixed * mixed, -1, keepdims=True)) + eps_norm)
    return (mixed * inverse).reshape(length, H * P_SIZE) * norm_gain
```

```python
import functools

import jax
import jax.numpy as jnp
from jax import lax
from jax.experimental import pallas as pl
from jax.experimental.pallas import tpu as pltpu
from jax.sharding import PartitionSpec as P

H = 128
P_SIZE = 64
N = 128
G = 8
CHUNK = 64
LANES = 256
EDGE = 8
PIECES = 3
MESH = pl.DeviceIdType.MESH
eps_norm = 1e-05
f32 = jnp.float32
bf16 = jnp.bfloat16


def split2(value):
    high = value.astype(bf16)
    return high, (value - high.astype(f32)).astype(bf16)


def split3(value):
    high = value.astype(bf16)
    rest = value - high.astype(f32)
    middle = rest.astype(bf16)
    return high, middle, (rest - middle.astype(f32)).astype(bf16)


def dot(a, b, dims=((1,), (0,))):
    return lax.dot_general(a, b, (dims, ((), ())), preferred_element_type=f32)


def dot3(a, b, dims=((1,), (0,))):
    return dot(a[0], b[0], dims) + (dot(a[0], b[1], dims) + dot(a[1], b[0], dims))


def silu(v):
    return v / (1.0 + jnp.exp(-v))


def conv(block, taps, extent):
    count = taps.shape[0]
    first = EDGE - (count - 1)
    summed = taps[0:1] * block[first : first + extent]
    for k in range(1, count):
        summed = summed + taps[k : k + 1] * block[first + k : first + k + extent]
    return silu(summed)


def kernel(
    nh,
    nc,
    x_hbm,
    w_hbm,
    r_hbm,
    l_hbm,
    cf_ref,
    cw_ref,
    cr_ref,
    out_hbm,
    xbuf,
    wbuf,
    rbuf,
    lbuf,
    yloc,
    cums,
    creads,
    gm,
    bt,
    sbuf,
    arecv,
    bsend,
    brecv,
    csend,
    crecv,
    dsend,
    inbuf,
    ysem,
    yrec,
    lsem,
    lrec,
    hsem,
    hrec,
    asem,
    arec,
    bsem,
    brec,
    csem,
    crec,
    dsem,
    drec,
    osem,
):
    c = lax.axis_index("ctx")
    h = lax.axis_index("head")
    groups = xbuf.shape[0]
    tl = x_hbm.shape[0]
    tokens = tl * nh
    width = xbuf.shape[2]
    heads_here = H // nh
    per_group = H // G
    core = c % 2
    side = (c // 2) % 2
    plane = c // 4
    planes = nc // 4
    core_peer = c + 1 - 2 * core
    side_peer = c + 2 - 4 * side

    barrier = pltpu.get_barrier_semaphore()

    def greet(ctx, head):
        pl.semaphore_signal(barrier, inc=1, device_id=(ctx, head), device_id_type=MESH)

    for d in range(1, nh):
        greet(c, (h + d) % nh)
    greet(core_peer, h)
    greet(side_peer, h)

    @pl.when(plane > 0)
    def _():
        greet(c - 4, h)

    @pl.when(plane < planes - 1)
    def _():
        greet(c + 4, h)

    @pl.when(c > 0)
    def _():
        greet(c - 1, nh - 1)

    gives_edge = jnp.logical_and(h == nh - 1, c < nc - 1)

    @pl.when(gives_edge)
    def _():
        for d in range(nh):
            greet(c + 1, d)

    below = (plane + planes - 1) // planes
    above = 1 - (plane + 1) // planes
    behind = (c + nc - 1) // nc
    ahead = ((h + 1) // nh) * (1 - (c + 1) // nc)
    pl.semaphore_wait(barrier, nh + 1 + below + above + behind + nh * ahead)

    kinds = ((x_hbm, xbuf, width), (w_hbm, wbuf, N), (r_hbm, rbuf, N))
    order = (1, 2, 0)

    def source(k, g, owner, start, rows):
        ref, _, wide = kinds[k]
        at = pl.multiple_of((owner * groups + g) * wide, wide)
        return ref.at[pl.ds(start, rows), pl.ds(at, wide)]

    def rows_of(owner):
        return pl.ds(pl.multiple_of(EDGE + owner * tl, 8), tl)

    def own_copy(k, g):
        return pltpu.make_async_copy(
            source(k, g, h, 0, tl), kinds[k][1].at[g, rows_of(h)], yrec.at[g, 0, k]
        )

    def head_copy(k, g, d, sender):
        return pltpu.make_async_remote_copy(
            src_ref=source(k, g, (h + d) % nh, 0, tl),
            dst_ref=kinds[k][1].at[g, rows_of(sender)],
            send_sem=ysem.at[g, d, k],
            recv_sem=yrec.at[g, d, k],
            device_id=(c, (h + d) % nh),
            device_id_type=MESH,
        )

    def decay_rows(owner):
        return lbuf.at[pl.ds(pl.multiple_of(owner * tl, 8), tl)]

    def decay_own():
        return pltpu.make_async_copy(l_hbm, decay_rows(h), lrec.at[0])

    def decay_copy(d, sender):
        return pltpu.make_async_remote_copy(
            src_ref=l_hbm,
            dst_ref=decay_rows(sender),
            send_sem=lsem.at[d],
            recv_sem=lrec.at[d],
            device_id=(c, (h + d) % nh),
            device_id_type=MESH,
        )

    def edge_copy(k, g, to):
        return pltpu.make_async_remote_copy(
            src_ref=source(k, g, to, tl - EDGE, EDGE),
            dst_ref=kinds[k][1].at[g, pl.ds(0, EDGE)],
            send_sem=hsem.at[g, to, k],
            recv_sem=hrec.at[g, k],
            device_id=(lax.rem(c + 1, nc), to),
            device_id_type=MESH,
        )

    decay_own().start()
    for d in range(1, nh):
        decay_copy(d, h).start()
    for g in range(groups):
        for k in order:
            own_copy(k, g).start()

        @pl.when(gives_edge)
        def _():
            for to in range(nh):
                for k in order:
                    edge_copy(k, g, to).start()

        for d in range(1, nh):
            for k in order:
                head_copy(k, g, d, h).start()

    @pl.when(c == 0)
    def _():
        for g in range(groups):
            for k in order:
                wide = kinds[k][2]
                kinds[k][1][g, 0:EDGE, :] = jnp.zeros((EDGE, wide), f32)

    decay_own().wait()
    for d in range(1, nh):
        decay_copy(d, (h - d + nh) % nh).wait_recv()
    target = lax.broadcasted_iota(jnp.int32, (tokens, tokens), 0)
    origin = lax.broadcasted_iota(jnp.int32, (tokens, tokens), 1)
    past = target >= origin
    near = jnp.logical_and(past, target // CHUNK == origin // CHUNK)
    decay3 = split3(lbuf[...])
    for which, mask in ((0, near), (1, past)):
        ones = jnp.where(mask, 1.0, 0.0).astype(bf16)
        total = dot(ones, decay3[0]) + dot(ones, decay3[1]) + dot(ones, decay3[2])
        for part, piece in enumerate(split3(total)):
            cums[which, part] = piece

    def spread(which, g, lane):
        head_at = lax.broadcasted_iota(jnp.int32, (H, LANES), 0)
        channel = lax.broadcasted_iota(jnp.int32, (H, LANES), 1)
        wanted = h * heads_here + g * per_group + (lane + channel) // P_SIZE
        ones = jnp.where(head_at == wanted, 1.0, 0.0).astype(bf16)
        return (
            dot(cums[which, 0], ones) + dot(cums[which, 1], ones) + dot(cums[which, 2], ones)
        )

    def peer_copy(src, dst, send, recv, ctx):
        return pltpu.make_async_remote_copy(
            src_ref=src,
            dst_ref=dst,
            send_sem=send,
            recv_sem=recv,
            device_id=(ctx, h),
            device_id_type=MESH,
        )

    piece_rows = sbuf.shape[2] // PIECES

    def rows_at(i):
        return pl.ds(i * piece_rows, piece_rows)

    def core_copy(g):
        return peer_copy(sbuf.at[g, 1 - core], arecv.at[g], asem.at[g], arec.at[g], core_peer)

    def side_copy(g, i):
        return peer_copy(
            bsend.at[g, rows_at(i)], brecv.at[g, rows_at(i)], bsem.at[g, i], brec.at[g, i], side_peer
        )

    def plane_copy(g, i):
        return peer_copy(
            csend.at[g, rows_at(i)],
            crecv.at[g, rows_at(i)],
            csem.at[g, i],
            crec.at[g, i],
            lax.rem(c + 4, nc),
        )

    def back_copy(g, i):
        return peer_copy(
            dsend.at[g, rows_at(i)],
            inbuf.at[g, core, rows_at(i)],
            dsem.at[g, i],
            drec.at[g, i],
            core_peer,
        )

    def back_arrival(g, i):
        return peer_copy(
            dsend.at[g, rows_at(i)],
            inbuf.at[g, 1 - core, rows_at(i)],
            dsem.at[g, i],
            drec.at[g, i],
            core_peer,
        )

    def local(g):
        for k in order:
            own_copy(k, g).wait()

        @pl.when(c > 0)
        def _():
            for k in order:
                edge_copy(k, g, 0).wait_recv()

        for d in range(1, nh):
            for k in order:
                head_copy(k, g, d, (h - d + nh) % nh).wait_recv()

        at = pl.multiple_of((h * groups + g) * N, N)
        writes = conv(wbuf[g], cw_ref[:, pl.ds(at, N)], tokens)
        reads = conv(rbuf[g], cr_ref[:, pl.ds(at, N)], tokens)
        reads2 = split2(reads)
        writes2 = split2(writes)
        creads[g, 0] = reads2[0]
        creads[g, 1] = reads2[1]
        row = lax.broadcasted_iota(jnp.int32, (CHUNK, CHUNK), 0)
        column = lax.broadcasted_iota(jnp.int32, (CHUNK, CHUNK), 1)
        for k in range(tokens // CHUNK):
            part = slice(k * CHUNK, (k + 1) * CHUNK)
            scores = dot3(
                (reads2[0][part], reads2[1][part]),
                (writes2[0][part], writes2[1][part]),
                ((1,), (1,)),
            )
            scores = split2(jnp.where(row >= column, scores, 0.0))
            gm[k, 0] = scores[0]
            gm[k, 1] = scores[1]
            turned = split2(jnp.transpose(writes[part]))
            bt[k, 0] = turned[0]
            bt[k, 1] = turned[1]

        def lanes(b, carry):
            lane = pl.multiple_of(b * LANES, LANES)
            cols = pl.ds(lane, LANES)
            taps = cf_ref[:, pl.ds(pl.multiple_of((h * groups + g) * width + lane, LANES), LANES)]
            spaced = spread(0, g, lane)
            state = None
            for k in range(tokens // CHUNK):
                part = slice(k * CHUNK, (k + 1) * CHUNK)
                act = conv(xbuf[g, k * CHUNK : k * CHUNK + CHUNK + EDGE, cols], taps, CHUNK)
                log = spaced[part]
                scaled = split2(act * jnp.exp(-log))
                mixed = dot3((gm[k, 0], gm[k, 1]), scaled)
                added = dot3((bt[k, 0], bt[k, 1]), scaled)
                if k > 0:
                    mixed = mixed + dot3((creads[g, 0, part], creads[g, 1, part]), split2(state))
                    added = added + state
                yloc[g, part, cols] = mixed * jnp.exp(log)
                state = added * jnp.exp(log[CHUNK - 1 : CHUNK])
            ends = spread(1, g, lane)[tokens - 1 : tokens]
            fade = jnp.broadcast_to(jnp.exp(ends), (EDGE, LANES))
            for half in range(2):
                sbuf[g, half, 0:EDGE, cols] = fade
                sbuf[g, half, EDGE : EDGE + N // 2, cols] = state[half * N // 2 : (half + 1) * N // 2]
            return carry

        lax.fori_loop(0, width // LANES, lanes, 0)
        core_copy(g).start()

    def pair(g):
        core_copy(g).wait_recv()
        mine_first = core == 0
        mine_fade = sbuf[g, core, 0:1]
        peer_fade = arecv[g, 0:1]
        late_fade = jnp.where(mine_first, peer_fade, mine_fade)
        for i in range(PIECES):
            rows = slice(i * piece_rows, (i + 1) * piece_rows)
            mine = sbuf[g, core, rows]
            peer = arecv[g, rows]
            first = jnp.where(mine_first, mine, peer)
            late = jnp.where(mine_first, peer, mine)
            bsend[g, rows] = late_fade * first + late
            if i == 0:
                bsend[g, 0:EDGE] = jnp.broadcast_to(mine_fade * peer_fade, (EDGE, width))
            side_copy(g, i).start()

    def chain(g):
        side_first = side == 0
        for i in range(PIECES):
            rows = slice(i * piece_rows, (i + 1) * piece_rows)
            side_copy(g, i).wait_recv()
            mine_fade = bsend[g, 0:1]
            peer_fade = brecv[g, 0:1]
            mine = bsend[g, rows]
            peer = brecv[g, rows]
            first = jnp.where(side_first, mine, peer)

            @pl.when(plane > 0)
            def _():
                plane_copy(g, i).wait_recv()

            @pl.when(plane == 0)
            def _():
                crecv[g, rows] = jnp.zeros((piece_rows, width), f32)

            entering = crecv[g, rows]

            @pl.when(plane < planes - 1)
            def _():
                late = jnp.where(side_first, peer, mine)
                late_fade = jnp.where(side_first, peer_fade, mine_fade)
                csend[g, rows] = (mine_fade * peer_fade) * entering + (late_fade * first + late)
                plane_copy(g, i).start()

            first_fade = jnp.where(side_first, mine_fade, peer_fade)
            even = jnp.where(side_first, entering, first_fade * entering + first)
            own = sbuf[g, core, rows]
            lead = jnp.where(core == 0, own, arecv[g, rows])
            lead_fade = jnp.where(core == 0, sbuf[g, core, 0:1], arecv[g, 0:1])
            odd = lead_fade * even + lead
            inbuf[g, core, rows] = jnp.where(core == 0, even, odd)
            dsend[g, rows] = jnp.where(core == 0, odd, even)
            back_copy(g, i).start()

    def out_copy(g):
        return pltpu.make_async_copy(
            yloc.at[g], out_hbm.at[:, pl.ds(pl.multiple_of(g * width, width), width)], osem.at[g]
        )

    def finish(g):
        for i in range(PIECES):
            back_arrival(g, i).wait_recv()

        def lanes(b, squares):
            lane = pl.multiple_of(b * LANES, LANES)
            cols = pl.ds(lane, LANES)
            state = jnp.concatenate(
                [
                    inbuf[g, 0, EDGE : EDGE + N // 2, cols],
                    inbuf[g, 1, EDGE : EDGE + N // 2, cols],
                ],
                0,
            )
            carried = dot3((creads[g, 0], creads[g, 1]), split2(state))
            mixed = yloc[g, :, cols] + carried * jnp.exp(spread(1, g, lane))
            yloc[g, :, cols] = mixed
            squared = mixed * mixed
            for at in range(0, LANES, 128):
                squares = squares + squared[:, at : at + 128]
            return squares

        squares = lax.fori_loop(0, width // LANES, lanes, jnp.zeros((tokens, 128), f32))
        inverse = lax.rsqrt(jnp.sum(squares, 1, keepdims=True) / width + eps_norm)
        yloc[g] = yloc[g] * inverse
        out_copy(g).start()

    def step(i, carry):
        @pl.when(i < groups)
        def _():
            local(i)
            pair(i)

        @pl.when(jnp.logical_and(i >= 1, i < groups + 1))
        def _():
            chain(i - 1)

        @pl.when(i >= 2)
        def _():
            finish(i - 2)

        return carry

    lax.fori_loop(0, groups + 2, step, 0)

    for d in range(1, nh):
        decay_copy(d, h).wait_send()
    for g in range(groups):
        out_copy(g).wait()
        core_copy(g).wait_send()
        for d in range(1, nh):
            for k in order:
                head_copy(k, g, d, h).wait_send()

        @pl.when(gives_edge)
        def _():
            for to in range(nh):
                for k in order:
                    edge_copy(k, g, to).wait_send()

        for i in range(PIECES):
            side_copy(g, i).wait_send()
            back_copy(g, i).wait_send()

            @pl.when(plane < planes - 1)
            def _():
                plane_copy(g, i).wait_send()


def shards(
    features, state_write, state_read, log_decay, conv_features, conv_write, conv_read, norm_gain
):
    nh = lax.axis_size("head")
    nc = lax.axis_size("ctx")
    groups = G // nh
    tokens = features.shape[0] * nh
    width = features.shape[1] // G
    half = N // 2 + EDGE
    count = tokens // CHUNK
    vm = pltpu.VMEM
    dma = pltpu.SemaphoreType.DMA
    anywhere = pl.BlockSpec(memory_space=pl.ANY)
    near = pl.BlockSpec(memory_space=pltpu.VMEM)
    mixed = pl.pallas_call(
        functools.partial(kernel, nh, nc),
        out_shape=jax.ShapeDtypeStruct((tokens, groups * width), f32),
        in_specs=[anywhere] * 4 + [near] * 3,
        out_specs=anywhere,
        scratch_shapes=[
            vm((groups, EDGE + tokens, width), f32),
            vm((groups, EDGE + tokens, N), f32),
            vm((groups, EDGE + tokens, N), f32),
            vm((tokens, H), f32),
            vm((groups, tokens, width), f32),
            vm((2, 3, tokens, H), bf16),
            vm((groups, 2, tokens, N), bf16),
            vm((count, 2, CHUNK, CHUNK), bf16),
            vm((count, 2, N, CHUNK), bf16),
            vm((groups, 2, half, width), f32),
            vm((groups, half, width), f32),
            vm((groups, half, width), f32),
            vm((groups, half, width), f32),
            vm((groups, half, width), f32),
            vm((groups, half, width), f32),
            vm((groups, half, width), f32),
            vm((groups, 2, half, width), f32),
            dma((groups, nh, 3)),
            dma((groups, nh, 3)),
            dma((nh,)),
            dma((nh,)),
            dma((groups, nh, 3)),
            dma((groups, 3)),
            dma((groups,)),
            dma((groups,)),
            dma((groups, PIECES)),
            dma((groups, PIECES)),
            dma((groups, PIECES)),
            dma((groups, PIECES)),
            dma((groups, PIECES)),
            dma((groups, PIECES)),
            dma((groups,)),
        ],
        compiler_params=pltpu.CompilerParams(
            collective_id=0, has_side_effects=True, vmem_limit_bytes=60 * 1024 * 1024
        ),
    )(features, state_write, state_read, log_decay, conv_features, conv_write, conv_read)
    return mixed * norm_gain


def solution(mesh):
    return jax.shard_map(
        shards,
        mesh=mesh,
        in_specs=(
            P(("ctx", "head"), None),
            P(("ctx", "head"), None),
            P(("ctx", "head"), None),
            P(("ctx", "head"), None),
            P(),
            P(),
            P(),
            P("head"),
        ),
        out_specs=P("ctx", "head"),
        check_vma=False,
    )
```

```python
import functools

import jax
import jax.numpy as jnp
from jax import lax
from jax.experimental import pallas as pl
from jax.experimental.pallas import tpu as pltpu
from jax.sharding import PartitionSpec as P

H = 128
P_SIZE = 64
N = 128
G = 8
CHUNK = 64
LANES = 256
EDGE = 8
PIECES = 3
PARTS = 2
MESH = pl.DeviceIdType.MESH
eps_norm = 1e-05
f32 = jnp.float32
bf16 = jnp.bfloat16


def split2(value):
    high = value.astype(bf16)
    return high, (value - high.astype(f32)).astype(bf16)


def split3(value):
    high = value.astype(bf16)
    rest = value - high.astype(f32)
    middle = rest.astype(bf16)
    return high, middle, (rest - middle.astype(f32)).astype(bf16)


def dot(a, b, dims=((1,), (0,))):
    return lax.dot_general(a, b, (dims, ((), ())), preferred_element_type=f32)


def dot3(a, b, dims=((1,), (0,))):
    return dot(a[0], b[0], dims) + (dot(a[0], b[1], dims) + dot(a[1], b[0], dims))


def silu(v):
    return v / (1.0 + jnp.exp(-v))


def conv(block, taps, extent):
    count = taps.shape[0]
    first = EDGE - (count - 1)
    summed = taps[0:1] * block[first : first + extent]
    for k in range(1, count):
        summed = summed + taps[k : k + 1] * block[first + k : first + k + extent]
    return silu(summed)


def kernel(
    nh,
    nc,
    x_hbm,
    w_hbm,
    r_hbm,
    l_hbm,
    cf_ref,
    cw_ref,
    cr_ref,
    out_hbm,
    xbuf,
    wbuf,
    rbuf,
    lbuf,
    yloc,
    cums,
    squares_ref,
    creads,
    gm,
    bt,
    sbuf,
    arecv,
    bsend,
    brecv,
    csend,
    crecv,
    dsend,
    inbuf,
    ysem,
    yrec,
    lsem,
    lrec,
    hsem,
    hrec,
    asem,
    arec,
    bsem,
    brec,
    csem,
    crec,
    dsem,
    drec,
    osem,
):
    c = lax.axis_index("ctx")
    h = lax.axis_index("head")
    units = xbuf.shape[0]
    groups = units // PARTS
    tl = x_hbm.shape[0]
    tokens = tl * nh
    width = xbuf.shape[2]
    heads_here = H // nh
    per_unit = H // G // PARTS
    core = c % 2
    side = (c // 2) % 2
    plane = c // 4
    planes = nc // 4
    core_peer = c + 1 - 2 * core
    side_peer = c + 2 - 4 * side

    barrier = pltpu.get_barrier_semaphore()

    def greet(ctx, head):
        pl.semaphore_signal(barrier, inc=1, device_id=(ctx, head), device_id_type=MESH)

    for d in range(1, nh):
        greet(c, (h + d) % nh)
    greet(core_peer, h)
    greet(side_peer, h)

    @pl.when(plane > 0)
    def _():
        greet(c - 4, h)

    @pl.when(plane < planes - 1)
    def _():
        greet(c + 4, h)

    @pl.when(c > 0)
    def _():
        greet(c - 1, nh - 1)

    gives_edge = jnp.logical_and(h == nh - 1, c < nc - 1)

    @pl.when(gives_edge)
    def _():
        for d in range(nh):
            greet(c + 1, d)

    below = (plane + planes - 1) // planes
    above = 1 - (plane + 1) // planes
    behind = (c + nc - 1) // nc
    ahead = ((h + 1) // nh) * (1 - (c + 1) // nc)
    pl.semaphore_wait(barrier, nh + 1 + below + above + behind + nh * ahead)

    kinds = ((x_hbm, xbuf, width), (w_hbm, wbuf, N), (r_hbm, rbuf, N))
    order = (1, 2, 0)

    def kinds_of(u):
        return order if u % PARTS == 0 else (0,)

    def slot(k, u):
        return u if k == 0 else u // PARTS

    def source(k, u, owner, start, rows):
        ref, _, wide = kinds[k]
        place = owner * units + u if k == 0 else owner * groups + u // PARTS
        at = pl.multiple_of(place * wide, wide)
        return ref.at[pl.ds(start, rows), pl.ds(at, wide)]

    def landing(k, u, rows):
        return kinds[k][1].at[slot(k, u), rows]

    def rows_of(owner):
        return pl.ds(pl.multiple_of(EDGE + owner * tl, 8), tl)

    def own_copy(k, g):
        return pltpu.make_async_copy(
            source(k, g, h, 0, tl), landing(k, g, rows_of(h)), yrec.at[g, 0, k]
        )

    def head_copy(k, g, d, sender):
        return pltpu.make_async_remote_copy(
            src_ref=source(k, g, (h + d) % nh, 0, tl),
            dst_ref=landing(k, g, rows_of(sender)),
            send_sem=ysem.at[g, d, k],
            recv_sem=yrec.at[g, d, k],
            device_id=(c, (h + d) % nh),
            device_id_type=MESH,
        )

    def decay_rows(owner):
        return lbuf.at[pl.ds(pl.multiple_of(owner * tl, 8), tl)]

    def decay_own():
        return pltpu.make_async_copy(l_hbm, decay_rows(h), lrec.at[0])

    def decay_copy(d, sender):
        return pltpu.make_async_remote_copy(
            src_ref=l_hbm,
            dst_ref=decay_rows(sender),
            send_sem=lsem.at[d],
            recv_sem=lrec.at[d],
            device_id=(c, (h + d) % nh),
            device_id_type=MESH,
        )

    def edge_copy(k, g, to):
        return pltpu.make_async_remote_copy(
            src_ref=source(k, g, to, tl - EDGE, EDGE),
            dst_ref=landing(k, g, pl.ds(0, EDGE)),
            send_sem=hsem.at[g, to, k],
            recv_sem=hrec.at[g, k],
            device_id=(lax.rem(c + 1, nc), to),
            device_id_type=MESH,
        )

    decay_own().start()
    for d in range(1, nh):
        decay_copy(d, h).start()
    for g in range(units):
        for k in kinds_of(g):
            own_copy(k, g).start()

        @pl.when(gives_edge)
        def _():
            for to in range(nh):
                for k in kinds_of(g):
                    edge_copy(k, g, to).start()

        for d in range(1, nh):
            for k in kinds_of(g):
                head_copy(k, g, d, h).start()

    @pl.when(c == 0)
    def _():
        for g in range(units):
            for k in kinds_of(g):
                wide = kinds[k][2]
                kinds[k][1][slot(k, g), 0:EDGE, :] = jnp.zeros((EDGE, wide), f32)

    decay_own().wait()
    for d in range(1, nh):
        decay_copy(d, (h - d + nh) % nh).wait_recv()
    target = lax.broadcasted_iota(jnp.int32, (tokens, tokens), 0)
    origin = lax.broadcasted_iota(jnp.int32, (tokens, tokens), 1)
    past = target >= origin
    near = jnp.logical_and(past, target // CHUNK == origin // CHUNK)
    decay3 = split3(lbuf[...])
    for which, mask in ((0, near), (1, past)):
        ones = jnp.where(mask, 1.0, 0.0).astype(bf16)
        total = dot(ones, decay3[0]) + dot(ones, decay3[1]) + dot(ones, decay3[2])
        for part, piece in enumerate(split3(total)):
            cums[which, part] = piece

    def spread(which, g, lane):
        head_at = lax.broadcasted_iota(jnp.int32, (H, LANES), 0)
        channel = lax.broadcasted_iota(jnp.int32, (H, LANES), 1)
        wanted = h * heads_here + g * per_unit + (lane + channel) // P_SIZE
        ones = jnp.where(head_at == wanted, 1.0, 0.0).astype(bf16)
        return (
            dot(cums[which, 0], ones) + dot(cums[which, 1], ones) + dot(cums[which, 2], ones)
        )

    def peer_copy(src, dst, send, recv, ctx):
        return pltpu.make_async_remote_copy(
            src_ref=src,
            dst_ref=dst,
            send_sem=send,
            recv_sem=recv,
            device_id=(ctx, h),
            device_id_type=MESH,
        )

    piece_rows = sbuf.shape[2] // PIECES

    def rows_at(i):
        return pl.ds(i * piece_rows, piece_rows)

    def core_copy(g):
        return peer_copy(sbuf.at[g, 1 - core], arecv.at[g], asem.at[g], arec.at[g], core_peer)

    def side_copy(g, i):
        return peer_copy(
            bsend.at[g, rows_at(i)], brecv.at[g, rows_at(i)], bsem.at[g, i], brec.at[g, i], side_peer
        )

    def plane_copy(g, i):
        return peer_copy(
            csend.at[g, rows_at(i)],
            crecv.at[g, rows_at(i)],
            csem.at[g, i],
            crec.at[g, i],
            lax.rem(c + 4, nc),
        )

    def back_copy(g, i):
        return peer_copy(
            dsend.at[g, rows_at(i)],
            inbuf.at[g, core, rows_at(i)],
            dsem.at[g, i],
            drec.at[g, i],
            core_peer,
        )

    def back_arrival(g, i):
        return peer_copy(
            dsend.at[g, rows_at(i)],
            inbuf.at[g, 1 - core, rows_at(i)],
            dsem.at[g, i],
            drec.at[g, i],
            core_peer,
        )

    def arrive(k, u):
        own_copy(k, u).wait()

        @pl.when(c > 0)
        def _():
            edge_copy(k, u, 0).wait_recv()

        for d in range(1, nh):
            head_copy(k, u, d, (h - d + nh) % nh).wait_recv()

    def project(u):
        g = u // PARTS
        for k in (1, 2):
            arrive(k, u)
        at = pl.multiple_of((h * groups + g) * N, N)
        writes = conv(wbuf[g], cw_ref[:, pl.ds(at, N)], tokens)
        reads = conv(rbuf[g], cr_ref[:, pl.ds(at, N)], tokens)
        reads2 = split2(reads)
        writes2 = split2(writes)
        creads[g, 0] = reads2[0]
        creads[g, 1] = reads2[1]
        row = lax.broadcasted_iota(jnp.int32, (CHUNK, CHUNK), 0)
        column = lax.broadcasted_iota(jnp.int32, (CHUNK, CHUNK), 1)
        for k in range(tokens // CHUNK):
            part = slice(k * CHUNK, (k + 1) * CHUNK)
            scores = dot3(
                (reads2[0][part], reads2[1][part]),
                (writes2[0][part], writes2[1][part]),
                ((1,), (1,)),
            )
            scores = split2(jnp.where(row >= column, scores, 0.0))
            gm[k, 0] = scores[0]
            gm[k, 1] = scores[1]
            turned = split2(jnp.transpose(writes[part]))
            bt[k, 0] = turned[0]
            bt[k, 1] = turned[1]

    def local(u):
        @pl.when(u % PARTS == 0)
        def _():
            project(u)

        g = u // PARTS
        arrive(0, u)

        def lanes(b, carry):
            lane = pl.multiple_of(b * LANES, LANES)
            cols = pl.ds(lane, LANES)
            taps = cf_ref[:, pl.ds(pl.multiple_of((h * units + u) * width + lane, LANES), LANES)]
            spaced = spread(0, u, lane)
            state = None
            for k in range(tokens // CHUNK):
                part = slice(k * CHUNK, (k + 1) * CHUNK)
                act = conv(xbuf[u, k * CHUNK : k * CHUNK + CHUNK + EDGE, cols], taps, CHUNK)
                log = spaced[part]
                scaled = split2(act * jnp.exp(-log))
                mixed = dot3((gm[k, 0], gm[k, 1]), scaled)
                added = dot3((bt[k, 0], bt[k, 1]), scaled)
                if k > 0:
                    mixed = mixed + dot3((creads[g, 0, part], creads[g, 1, part]), split2(state))
                    added = added + state
                yloc[u, part, cols] = mixed * jnp.exp(log)
                state = added * jnp.exp(log[CHUNK - 1 : CHUNK])
            ends = spread(1, u, lane)[tokens - 1 : tokens]
            fade = jnp.broadcast_to(jnp.exp(ends), (EDGE, LANES))
            for half in range(2):
                sbuf[u, half, 0:EDGE, cols] = fade
                sbuf[u, half, EDGE : EDGE + N // 2, cols] = state[half * N // 2 : (half + 1) * N // 2]
            return carry

        lax.fori_loop(0, width // LANES, lanes, 0)
        core_copy(u).start()

    def pair(g):
        core_copy(g).wait_recv()
        mine_first = core == 0
        mine_fade = sbuf[g, core, 0:1]
        peer_fade = arecv[g, 0:1]
        late_fade = jnp.where(mine_first, peer_fade, mine_fade)
        for i in range(PIECES):
            rows = slice(i * piece_rows, (i + 1) * piece_rows)
            mine = sbuf[g, core, rows]
            peer = arecv[g, rows]
            first = jnp.where(mine_first, mine, peer)
            late = jnp.where(mine_first, peer, mine)
            bsend[g, rows] = late_fade * first + late
            if i == 0:
                bsend[g, 0:EDGE] = jnp.broadcast_to(mine_fade * peer_fade, (EDGE, width))
            side_copy(g, i).start()

    def chain(g):
        side_first = side == 0
        for i in range(PIECES):
            rows = slice(i * piece_rows, (i + 1) * piece_rows)
            side_copy(g, i).wait_recv()
            mine_fade = bsend[g, 0:1]
            peer_fade = brecv[g, 0:1]
            mine = bsend[g, rows]
            peer = brecv[g, rows]
            first = jnp.where(side_first, mine, peer)

            @pl.when(plane > 0)
            def _():
                plane_copy(g, i).wait_recv()

            @pl.when(plane == 0)
            def _():
                crecv[g, rows] = jnp.zeros((piece_rows, width), f32)

            entering = crecv[g, rows]

            @pl.when(plane < planes - 1)
            def _():
                late = jnp.where(side_first, peer, mine)
                late_fade = jnp.where(side_first, peer_fade, mine_fade)
                csend[g, rows] = (mine_fade * peer_fade) * entering + (late_fade * first + late)
                plane_copy(g, i).start()

            first_fade = jnp.where(side_first, mine_fade, peer_fade)
            even = jnp.where(side_first, entering, first_fade * entering + first)
            own = sbuf[g, core, rows]
            lead = jnp.where(core == 0, own, arecv[g, rows])
            lead_fade = jnp.where(core == 0, sbuf[g, core, 0:1], arecv[g, 0:1])
            odd = lead_fade * even + lead
            inbuf[g, core, rows] = jnp.where(core == 0, even, odd)
            dsend[g, rows] = jnp.where(core == 0, odd, even)
            back_copy(g, i).start()

    def out_copy(g):
        return pltpu.make_async_copy(
            yloc.at[g], out_hbm.at[:, pl.ds(pl.multiple_of(g * width, width), width)], osem.at[g]
        )

    def finish(u):
        g = u // PARTS
        for i in range(PIECES):
            back_arrival(u, i).wait_recv()

        def lanes(b, squares):
            lane = pl.multiple_of(b * LANES, LANES)
            cols = pl.ds(lane, LANES)
            state = jnp.concatenate(
                [
                    inbuf[u, 0, EDGE : EDGE + N // 2, cols],
                    inbuf[u, 1, EDGE : EDGE + N // 2, cols],
                ],
                0,
            )
            carried = dot3((creads[g, 0], creads[g, 1]), split2(state))
            mixed = yloc[u, :, cols] + carried * jnp.exp(spread(1, u, lane))
            yloc[u, :, cols] = mixed
            squared = mixed * mixed
            for at in range(0, LANES, 128):
                squares = squares + squared[:, at : at + 128]
            return squares

        before = jnp.where(u % PARTS == 0, 0.0, 1.0) * squares_ref[...]
        squares_ref[...] = lax.fori_loop(0, width // LANES, lanes, before)

        @pl.when(u % PARTS == PARTS - 1)
        def _():
            mean = jnp.sum(squares_ref[...], 1, keepdims=True) / (width * PARTS)
            inverse = lax.rsqrt(mean + eps_norm)
            for back in range(PARTS - 1, -1, -1):
                yloc[u - back] = yloc[u - back] * inverse
                out_copy(u - back).start()

    def step(i, carry):
        @pl.when(i < units)
        def _():
            local(i)
            pair(i)

        @pl.when(i >= 2)
        def _():
            finish(i - 2)

        @pl.when(jnp.logical_and(i >= 1, i < units + 1))
        def _():
            chain(i - 1)

        return carry

    squares_ref[...] = jnp.zeros((tokens, 128), f32)
    lax.fori_loop(0, units + 2, step, 0)

    for d in range(1, nh):
        decay_copy(d, h).wait_send()
    for g in range(units):
        out_copy(g).wait()
        core_copy(g).wait_send()
        for d in range(1, nh):
            for k in kinds_of(g):
                head_copy(k, g, d, h).wait_send()

        @pl.when(gives_edge)
        def _():
            for to in range(nh):
                for k in kinds_of(g):
                    edge_copy(k, g, to).wait_send()

        for i in range(PIECES):
            side_copy(g, i).wait_send()
            back_copy(g, i).wait_send()

            @pl.when(plane < planes - 1)
            def _():
                plane_copy(g, i).wait_send()


def shards(
    features, state_write, state_read, log_decay, conv_features, conv_write, conv_read, norm_gain
):
    nh = lax.axis_size("head")
    nc = lax.axis_size("ctx")
    groups = G // nh
    units = groups * PARTS
    tokens = features.shape[0] * nh
    width = features.shape[1] // (G * PARTS)
    half = N // 2 + EDGE
    count = tokens // CHUNK
    vm = pltpu.VMEM
    dma = pltpu.SemaphoreType.DMA
    anywhere = pl.BlockSpec(memory_space=pl.ANY)
    near = pl.BlockSpec(memory_space=pltpu.VMEM)
    mixed = pl.pallas_call(
        functools.partial(kernel, nh, nc),
        out_shape=jax.ShapeDtypeStruct((tokens, units * width), f32),
        in_specs=[anywhere] * 4 + [near] * 3,
        out_specs=anywhere,
        scratch_shapes=[
            vm((units, EDGE + tokens, width), f32),
            vm((groups, EDGE + tokens, N), f32),
            vm((groups, EDGE + tokens, N), f32),
            vm((tokens, H), f32),
            vm((units, tokens, width), f32),
            vm((2, 3, tokens, H), bf16),
            vm((tokens, 128), f32),
            vm((groups, 2, tokens, N), bf16),
            vm((count, 2, CHUNK, CHUNK), bf16),
            vm((count, 2, N, CHUNK), bf16),
            vm((units, 2, half, width), f32),
            vm((units, half, width), f32),
            vm((units, half, width), f32),
            vm((units, half, width), f32),
            vm((units, half, width), f32),
            vm((units, half, width), f32),
            vm((units, half, width), f32),
            vm((units, 2, half, width), f32),
            dma((units, nh, 3)),
            dma((units, nh, 3)),
            dma((nh,)),
            dma((nh,)),
            dma((units, nh, 3)),
            dma((units, 3)),
            dma((units,)),
            dma((units,)),
            dma((units, PIECES)),
            dma((units, PIECES)),
            dma((units, PIECES)),
            dma((units, PIECES)),
            dma((units, PIECES)),
            dma((units, PIECES)),
            dma((units,)),
        ],
        compiler_params=pltpu.CompilerParams(
            collective_id=0, has_side_effects=True, vmem_limit_bytes=60 * 1024 * 1024
        ),
    )(features, state_write, state_read, log_decay, conv_features, conv_write, conv_read)
    return mixed * norm_gain


def solution(mesh):
    return jax.shard_map(
        shards,
        mesh=mesh,
        in_specs=(
            P(("ctx", "head"), None),
            P(("ctx", "head"), None),
            P(("ctx", "head"), None),
            P(("ctx", "head"), None),
            P(),
            P(),
            P(),
            P("head"),
        ),
        out_specs=P("ctx", "head"),
        check_vma=False,
    )
```

```python
import functools

import jax
import jax.numpy as jnp
from jax import lax
from jax.experimental import pallas as pl
from jax.experimental.pallas import tpu as pltpu
from jax.sharding import PartitionSpec as P

H = 128
P_SIZE = 64
N = 128
G = 8
CHUNK = 64
LANES = 256
EDGE = 8
PIECES = 9
PARTS = 2
MESH = pl.DeviceIdType.MESH
eps_norm = 1e-05
f32 = jnp.float32
bf16 = jnp.bfloat16


def split2(value):
    high = value.astype(bf16)
    return high, (value - high.astype(f32)).astype(bf16)


def split3(value):
    high = value.astype(bf16)
    rest = value - high.astype(f32)
    middle = rest.astype(bf16)
    return high, middle, (rest - middle.astype(f32)).astype(bf16)


def dot(a, b, dims=((1,), (0,))):
    return lax.dot_general(a, b, (dims, ((), ())), preferred_element_type=f32)


def dot3(a, b, dims=((1,), (0,))):
    return dot(a[0], b[0], dims) + (dot(a[0], b[1], dims) + dot(a[1], b[0], dims))


def silu(v):
    return v / (1.0 + jnp.exp(-v))


def conv(block, taps, extent):
    count = taps.shape[0]
    first = EDGE - (count - 1)
    summed = taps[0:1] * block[first : first + extent]
    for k in range(1, count):
        summed = summed + taps[k : k + 1] * block[first + k : first + k + extent]
    return silu(summed)


def kernel(
    nh,
    nc,
    x_hbm,
    w_hbm,
    r_hbm,
    l_hbm,
    cf_ref,
    cw_ref,
    cr_ref,
    out_ref,
    xbuf,
    wbuf,
    rbuf,
    lbuf,
    yloc,
    cums,
    squares_ref,
    creads,
    gm,
    bt,
    sbuf,
    arecv,
    bsend,
    brecv,
    csend,
    crecv,
    dsend,
    inbuf,
    ysem,
    yrec,
    lsem,
    lrec,
    hsem,
    hrec,
    asem,
    arec,
    bsem,
    brec,
    csem,
    crec,
    dsem,
    drec,
):
    c = lax.axis_index("ctx")
    h = lax.axis_index("head")
    units = xbuf.shape[0]
    groups = units // PARTS
    tl = x_hbm.shape[0]
    tokens = tl * nh
    width = xbuf.shape[2]
    heads_here = H // nh
    per_unit = H // G // PARTS
    core = c % 2
    side = (c // 2) % 2
    plane = c // 4
    planes = nc // 4
    core_peer = c + 1 - 2 * core
    side_peer = c + 2 - 4 * side

    barrier = pltpu.get_barrier_semaphore()

    def greet(ctx, head):
        pl.semaphore_signal(barrier, inc=1, device_id=(ctx, head), device_id_type=MESH)

    for d in range(1, nh):
        greet(c, (h + d) % nh)
    greet(core_peer, h)
    greet(side_peer, h)

    @pl.when(plane > 0)
    def _():
        greet(c - 4, h)

    @pl.when(plane < planes - 1)
    def _():
        greet(c + 4, h)

    @pl.when(c > 0)
    def _():
        greet(c - 1, h)

    gives_edge = c < nc - 1

    @pl.when(gives_edge)
    def _():
        greet(c + 1, h)

    below = (plane + planes - 1) // planes
    above = 1 - (plane + 1) // planes
    behind = (c + nc - 1) // nc
    ahead = 1 - (c + 1) // nc
    pl.semaphore_wait(barrier, nh + 1 + below + above + behind + ahead)

    kinds = ((x_hbm, xbuf, width), (w_hbm, wbuf, N), (r_hbm, rbuf, N))
    order = (1, 2, 0)

    def kinds_of(u):
        return order if u % PARTS == 0 else (0,)

    def slot(k, u):
        return u if k == 0 else u // PARTS

    def source(k, u, owner, start, rows):
        ref, _, wide = kinds[k]
        place = owner * units + u if k == 0 else owner * groups + u // PARTS
        at = pl.multiple_of(place * wide, wide)
        return ref.at[pl.ds(start, rows), pl.ds(at, wide)]

    def landing(k, u, rows):
        return kinds[k][1].at[slot(k, u), rows]

    def rows_of(owner, edge):
        start = EDGE + owner * tl + edge * (tl - EDGE)
        return pl.ds(pl.multiple_of(start, 8), EDGE if edge else tl - EDGE)

    def taken(k, u, owner, edge):
        return source(k, u, owner, edge * (tl - EDGE), EDGE if edge else tl - EDGE)

    def own_copy(k, u, edge):
        return pltpu.make_async_copy(
            taken(k, u, h, edge), landing(k, u, rows_of(h, edge)), yrec.at[u, 0, k + 3 * edge]
        )

    def head_copy(k, u, d, sender, edge):
        return pltpu.make_async_remote_copy(
            src_ref=taken(k, u, (h + d) % nh, edge),
            dst_ref=landing(k, u, rows_of(sender, edge)),
            send_sem=ysem.at[u, d, k + 3 * edge],
            recv_sem=yrec.at[u, d, k + 3 * edge],
            device_id=(c, (h + d) % nh),
            device_id_type=MESH,
        )

    def decay_rows(owner):
        return lbuf.at[pl.ds(pl.multiple_of(owner * tl, 8), tl)]

    def decay_own():
        return pltpu.make_async_copy(l_hbm, decay_rows(h), lrec.at[0])

    def decay_copy(d, sender):
        return pltpu.make_async_remote_copy(
            src_ref=l_hbm,
            dst_ref=decay_rows(sender),
            send_sem=lsem.at[d],
            recv_sem=lrec.at[d],
            device_id=(c, (h + d) % nh),
            device_id_type=MESH,
        )

    def edge_copy(k, u):
        return pltpu.make_async_remote_copy(
            src_ref=landing(k, u, pl.ds(tokens, EDGE)),
            dst_ref=landing(k, u, pl.ds(0, EDGE)),
            send_sem=hsem.at[u, k],
            recv_sem=hrec.at[u, k],
            device_id=(lax.rem(c + 1, nc), h),
            device_id_type=MESH,
        )

    decay_own().start()
    for d in range(1, nh):
        decay_copy(d, h).start()
    for edge in (1, 0):
        for u in range(units):
            for k in kinds_of(u):
                own_copy(k, u, edge).start()
                for d in range(1, nh):
                    head_copy(k, u, d, h, edge).start()

    @pl.when(c == 0)
    def _():
        for g in range(units):
            for k in kinds_of(g):
                wide = kinds[k][2]
                kinds[k][1][slot(k, g), 0:EDGE, :] = jnp.zeros((EDGE, wide), f32)

    decay_own().wait()
    for d in range(1, nh):
        decay_copy(d, (h - d + nh) % nh).wait_recv()
    target = lax.broadcasted_iota(jnp.int32, (tokens, tokens), 0)
    origin = lax.broadcasted_iota(jnp.int32, (tokens, tokens), 1)
    past = target >= origin
    near = jnp.logical_and(past, target // CHUNK == origin // CHUNK)
    decay3 = split3(lbuf[...])
    for which, mask in ((0, near), (1, past)):
        ones = jnp.where(mask, 1.0, 0.0).astype(bf16)
        total = dot(ones, decay3[0]) + dot(ones, decay3[1]) + dot(ones, decay3[2])
        for part, piece in enumerate(split3(total)):
            cums[which, part] = piece

    last = (h + 1) % nh
    for u in range(units):
        for k in kinds_of(u):

            @pl.when(h == nh - 1)
            def _():
                own_copy(k, u, 1).wait()

            @pl.when(h < nh - 1)
            def _():
                head_copy(k, u, last, nh - 1, 1).wait_recv()

            @pl.when(gives_edge)
            def _():
                edge_copy(k, u).start()

    def spread(which, g, lane):
        head_at = lax.broadcasted_iota(jnp.int32, (H, LANES), 0)
        channel = lax.broadcasted_iota(jnp.int32, (H, LANES), 1)
        wanted = h * heads_here + g * per_unit + (lane + channel) // P_SIZE
        ones = jnp.where(head_at == wanted, 1.0, 0.0).astype(bf16)
        return (
            dot(cums[which, 0], ones) + dot(cums[which, 1], ones) + dot(cums[which, 2], ones)
        )

    def peer_copy(src, dst, send, recv, ctx):
        return pltpu.make_async_remote_copy(
            src_ref=src,
            dst_ref=dst,
            send_sem=send,
            recv_sem=recv,
            device_id=(ctx, h),
            device_id_type=MESH,
        )

    piece_rows = sbuf.shape[2] // PIECES

    def rows_at(i):
        return pl.ds(i * piece_rows, piece_rows)

    def core_copy(g):
        return peer_copy(sbuf.at[g, 1 - core], arecv.at[g], asem.at[g], arec.at[g], core_peer)

    def side_copy(g, i):
        return peer_copy(
            bsend.at[g, rows_at(i)], brecv.at[g, rows_at(i)], bsem.at[g, i], brec.at[g, i], side_peer
        )

    def plane_copy(g, i):
        return peer_copy(
            csend.at[g, rows_at(i)],
            crecv.at[g, rows_at(i)],
            csem.at[g, i],
            crec.at[g, i],
            lax.rem(c + 4, nc),
        )

    def back_copy(g, i):
        return peer_copy(
            dsend.at[g, rows_at(i)],
            inbuf.at[g, core, rows_at(i)],
            dsem.at[g, i],
            drec.at[g, i],
            core_peer,
        )

    def back_arrival(g, i):
        return peer_copy(
            dsend.at[g, rows_at(i)],
            inbuf.at[g, 1 - core, rows_at(i)],
            dsem.at[g, i],
            drec.at[g, i],
            core_peer,
        )

    def arrive(k, u):
        own_copy(k, u, 0).wait()

        @pl.when(c > 0)
        def _():
            edge_copy(k, u).wait_recv()

        @pl.when(h < nh - 1)
        def _():
            own_copy(k, u, 1).wait()

        for d in range(1, nh):
            head_copy(k, u, d, (h - d + nh) % nh, 0).wait_recv()

            @pl.when(d != last)
            def _():
                head_copy(k, u, d, (h - d + nh) % nh, 1).wait_recv()

    def project(u):
        g = u // PARTS
        for k in (1, 2):
            arrive(k, u)
        at = pl.multiple_of((h * groups + g) * N, N)
        writes = conv(wbuf[g], cw_ref[:, pl.ds(at, N)], tokens)
        reads = conv(rbuf[g], cr_ref[:, pl.ds(at, N)], tokens)
        reads2 = split2(reads)
        writes2 = split2(writes)
        creads[g, 0] = reads2[0]
        creads[g, 1] = reads2[1]
        row = lax.broadcasted_iota(jnp.int32, (CHUNK, CHUNK), 0)
        column = lax.broadcasted_iota(jnp.int32, (CHUNK, CHUNK), 1)
        for k in range(tokens // CHUNK):
            part = slice(k * CHUNK, (k + 1) * CHUNK)
            scores = dot3(
                (reads2[0][part], reads2[1][part]),
                (writes2[0][part], writes2[1][part]),
                ((1,), (1,)),
            )
            scores = split2(jnp.where(row >= column, scores, 0.0))
            gm[k, 0] = scores[0]
            gm[k, 1] = scores[1]
            turned = split2(jnp.transpose(writes[part]))
            bt[k, 0] = turned[0]
            bt[k, 1] = turned[1]

    def local(u):
        @pl.when(u % PARTS == 0)
        def _():
            project(u)

        g = u // PARTS
        arrive(0, u)

        def lanes(b, carry):
            lane = pl.multiple_of(b * LANES, LANES)
            cols = pl.ds(lane, LANES)
            taps = cf_ref[:, pl.ds(pl.multiple_of((h * units + u) * width + lane, LANES), LANES)]
            spaced = spread(0, u, lane)
            state = None
            for k in range(tokens // CHUNK):
                part = slice(k * CHUNK, (k + 1) * CHUNK)
                act = conv(xbuf[u, k * CHUNK : k * CHUNK + CHUNK + EDGE, cols], taps, CHUNK)
                log = spaced[part]
                scaled = split2(act * jnp.exp(-log))
                mixed = dot3((gm[k, 0], gm[k, 1]), scaled)
                added = dot3((bt[k, 0], bt[k, 1]), scaled)
                if k > 0:
                    mixed = mixed + dot3((creads[g, 0, part], creads[g, 1, part]), split2(state))
                    added = added + state
                yloc[u, part, cols] = mixed * jnp.exp(log)
                state = added * jnp.exp(log[CHUNK - 1 : CHUNK])
            ends = spread(1, u, lane)[tokens - 1 : tokens]
            fade = jnp.broadcast_to(jnp.exp(ends), (EDGE, LANES))
            for half in range(2):
                sbuf[u, half, 0:EDGE, cols] = fade
                sbuf[u, half, EDGE : EDGE + N // 2, cols] = state[half * N // 2 : (half + 1) * N // 2]
            return carry

        lax.fori_loop(0, width // LANES, lanes, 0)
        core_copy(u).start()

    def pair(g):
        core_copy(g).wait_recv()
        mine_first = core == 0
        mine_fade = sbuf[g, core, 0:1]
        peer_fade = arecv[g, 0:1]
        late_fade = jnp.where(mine_first, peer_fade, mine_fade)
        for i in range(PIECES):
            rows = slice(i * piece_rows, (i + 1) * piece_rows)
            mine = sbuf[g, core, rows]
            peer = arecv[g, rows]
            first = jnp.where(mine_first, mine, peer)
            late = jnp.where(mine_first, peer, mine)
            bsend[g, rows] = late_fade * first + late
            if i == 0:
                bsend[g, 0:EDGE] = jnp.broadcast_to(mine_fade * peer_fade, (EDGE, width))
            side_copy(g, i).start()

    def chain(g):
        side_first = side == 0
        for i in range(PIECES):
            rows = slice(i * piece_rows, (i + 1) * piece_rows)
            side_copy(g, i).wait_recv()
            mine_fade = bsend[g, 0:1]
            peer_fade = brecv[g, 0:1]
            mine = bsend[g, rows]
            peer = brecv[g, rows]
            first = jnp.where(side_first, mine, peer)

            @pl.when(plane > 0)
            def _():
                plane_copy(g, i).wait_recv()

            @pl.when(plane == 0)
            def _():
                crecv[g, rows] = jnp.zeros((piece_rows, width), f32)

            entering = crecv[g, rows]

            @pl.when(plane < planes - 1)
            def _():
                late = jnp.where(side_first, peer, mine)
                late_fade = jnp.where(side_first, peer_fade, mine_fade)
                csend[g, rows] = (mine_fade * peer_fade) * entering + (late_fade * first + late)
                plane_copy(g, i).start()

            first_fade = jnp.where(side_first, mine_fade, peer_fade)
            even = jnp.where(side_first, entering, first_fade * entering + first)
            own = sbuf[g, core, rows]
            lead = jnp.where(core == 0, own, arecv[g, rows])
            lead_fade = jnp.where(core == 0, sbuf[g, core, 0:1], arecv[g, 0:1])
            odd = lead_fade * even + lead
            inbuf[g, core, rows] = jnp.where(core == 0, even, odd)
            dsend[g, rows] = jnp.where(core == 0, odd, even)
            back_copy(g, i).start()

    def finish(u):
        g = u // PARTS
        for i in range(PIECES):
            back_arrival(u, i).wait_recv()

        def lanes(b, squares):
            lane = pl.multiple_of(b * LANES, LANES)
            cols = pl.ds(lane, LANES)
            state = jnp.concatenate(
                [
                    inbuf[u, 0, EDGE : EDGE + N // 2, cols],
                    inbuf[u, 1, EDGE : EDGE + N // 2, cols],
                ],
                0,
            )
            carried = dot3((creads[g, 0], creads[g, 1]), split2(state))
            mixed = yloc[u, :, cols] + carried * jnp.exp(spread(1, u, lane))
            yloc[u, :, cols] = mixed
            squared = mixed * mixed
            for at in range(0, LANES, 128):
                squares = squares + squared[:, at : at + 128]
            return squares

        before = jnp.where(u % PARTS == 0, 0.0, 1.0) * squares_ref[...]
        squares_ref[...] = lax.fori_loop(0, width // LANES, lanes, before)

        @pl.when(u % PARTS == PARTS - 1)
        def _():
            mean = jnp.sum(squares_ref[...], 1, keepdims=True) / (width * PARTS)
            inverse = lax.rsqrt(mean + eps_norm)
            for back in range(PARTS - 1, -1, -1):
                cols = pl.ds(pl.multiple_of((u - back) * width, width), width)
                out_ref[:, cols] = yloc[u - back] * inverse

    def step(i, carry):
        @pl.when(i < units)
        def _():
            local(i)
            pair(i)

        @pl.when(i >= 2)
        def _():
            finish(i - 2)

        @pl.when(jnp.logical_and(i >= 1, i < units + 1))
        def _():
            chain(i - 1)

        return carry

    squares_ref[...] = jnp.zeros((tokens, 128), f32)
    lax.fori_loop(0, units + 2, step, 0)

    for d in range(1, nh):
        decay_copy(d, h).wait_send()
    for g in range(units):
        core_copy(g).wait_send()
        for d in range(1, nh):
            for k in kinds_of(g):
                head_copy(k, g, d, h, 0).wait_send()
                head_copy(k, g, d, h, 1).wait_send()

        @pl.when(gives_edge)
        def _():
            for k in kinds_of(g):
                edge_copy(k, g).wait_send()

        for i in range(PIECES):
            side_copy(g, i).wait_send()
            back_copy(g, i).wait_send()

            @pl.when(plane < planes - 1)
            def _():
                plane_copy(g, i).wait_send()


def shards(
    features, state_write, state_read, log_decay, conv_features, conv_write, conv_read, norm_gain
):
    nh = lax.axis_size("head")
    nc = lax.axis_size("ctx")
    groups = G // nh
    units = groups * PARTS
    tokens = features.shape[0] * nh
    width = features.shape[1] // (G * PARTS)
    half = N // 2 + EDGE
    count = tokens // CHUNK
    vm = pltpu.VMEM
    dma = pltpu.SemaphoreType.DMA
    anywhere = pl.BlockSpec(memory_space=pl.ANY)
    near = pl.BlockSpec(memory_space=pltpu.VMEM)
    mixed = pl.pallas_call(
        functools.partial(kernel, nh, nc),
        out_shape=pltpu.VMEM((tokens, units * width), f32),
        in_specs=[anywhere] * 4 + [near] * 3,
        out_specs=near,
        scratch_shapes=[
            vm((units, EDGE + tokens, width), f32),
            vm((groups, EDGE + tokens, N), f32),
            vm((groups, EDGE + tokens, N), f32),
            vm((tokens, H), f32),
            vm((units, tokens, width), f32),
            vm((2, 3, tokens, H), bf16),
            vm((tokens, 128), f32),
            vm((groups, 2, tokens, N), bf16),
            vm((count, 2, CHUNK, CHUNK), bf16),
            vm((count, 2, N, CHUNK), bf16),
            vm((units, 2, half, width), f32),
            vm((units, half, width), f32),
            vm((units, half, width), f32),
            vm((units, half, width), f32),
            vm((units, half, width), f32),
            vm((units, half, width), f32),
            vm((units, half, width), f32),
            vm((units, 2, half, width), f32),
            dma((units, nh, 6)),
            dma((units, nh, 6)),
            dma((nh,)),
            dma((nh,)),
            dma((units, 3)),
            dma((units, 3)),
            dma((units,)),
            dma((units,)),
            dma((units, PIECES)),
            dma((units, PIECES)),
            dma((units, PIECES)),
            dma((units, PIECES)),
            dma((units, PIECES)),
            dma((units, PIECES)),
        ],
        compiler_params=pltpu.CompilerParams(
            collective_id=0, has_side_effects=True, vmem_limit_bytes=58 * 1024 * 1024
        ),
    )(features, state_write, state_read, log_decay, conv_features, conv_write, conv_read)
    return mixed * norm_gain


def solution(mesh):
    return jax.shard_map(
        shards,
        mesh=mesh,
        in_specs=(
            P(("ctx", "head"), None),
            P(("ctx", "head"), None),
            P(("ctx", "head"), None),
            P(("ctx", "head"), None),
            P(),
            P(),
            P(),
            P("head"),
        ),
        out_specs=P("ctx", "head"),
        check_vma=False,
    )
```

```python
import functools

import jax
import jax.numpy as jnp
from jax import lax
from jax.experimental import pallas as pl
from jax.experimental.pallas import tpu as pltpu
from jax.sharding import PartitionSpec as P

H = 128
P_SIZE = 64
N = 128
G = 8
CHUNK = 64
LANES = 256
EDGE = 8
PIECES = 3
PARTS = 2
MESH = pl.DeviceIdType.MESH
eps_norm = 1e-05
f32 = jnp.float32
bf16 = jnp.bfloat16


def split2(value):
    high = value.astype(bf16)
    return high, (value - high.astype(f32)).astype(bf16)


def split3(value):
    high = value.astype(bf16)
    rest = value - high.astype(f32)
    middle = rest.astype(bf16)
    return high, middle, (rest - middle.astype(f32)).astype(bf16)


def dot(a, b, dims=((1,), (0,))):
    return lax.dot_general(a, b, (dims, ((), ())), preferred_element_type=f32)


def dot3(a, b, dims=((1,), (0,))):
    return dot(a[0], b[0], dims) + (dot(a[0], b[1], dims) + dot(a[1], b[0], dims))


def silu(v):
    return v / (1.0 + jnp.exp(-v))


def conv(block, taps, extent):
    count = taps.shape[0]
    first = EDGE - (count - 1)
    summed = taps[0:1] * block[first : first + extent]
    for k in range(1, count):
        summed = summed + taps[k : k + 1] * block[first + k : first + k + extent]
    return silu(summed)


def kernel(
    nh,
    nc,
    x_hbm,
    w_hbm,
    r_hbm,
    l_hbm,
    cf_ref,
    cw_ref,
    cr_ref,
    out_ref,
    xbuf,
    wbuf,
    rbuf,
    lbuf,
    yloc,
    cums,
    squares_ref,
    creads,
    gm,
    bt,
    sbuf,
    arecv,
    bsend,
    brecv,
    csend,
    crecv,
    dsend,
    inbuf,
    ysem,
    yrec,
    lsem,
    lrec,
    hsem,
    hrec,
    asem,
    arec,
    bsem,
    brec,
    csem,
    crec,
    dsem,
    drec,
):
    c = lax.axis_index("ctx")
    h = lax.axis_index("head")
    units = xbuf.shape[0]
    groups = units // PARTS
    tl = x_hbm.shape[0]
    tokens = tl * nh
    width = xbuf.shape[2]
    heads_here = H // nh
    per_unit = H // G // PARTS
    core = c % 2
    side = (c // 2) % 2
    plane = c // 4
    planes = nc // 4
    core_peer = c + 1 - 2 * core
    side_peer = c + 2 - 4 * side

    barrier = pltpu.get_barrier_semaphore()

    def greet(ctx, head):
        pl.semaphore_signal(barrier, inc=1, device_id=(ctx, head), device_id_type=MESH)

    for d in range(1, nh):
        greet(c, (h + d) % nh)
    greet(core_peer, h)
    greet(side_peer, h)

    @pl.when(plane > 0)
    def _():
        greet(c - 4, h)

    @pl.when(plane < planes - 1)
    def _():
        greet(c + 4, h)

    @pl.when(c > 0)
    def _():
        greet(c - 1, h)

    gives_edge = c < nc - 1

    @pl.when(gives_edge)
    def _():
        greet(c + 1, h)

    below = (plane + planes - 1) // planes
    above = 1 - (plane + 1) // planes
    behind = (c + nc - 1) // nc
    ahead = 1 - (c + 1) // nc
    pl.semaphore_wait(barrier, nh + 1 + below + above + behind + ahead)

    kinds = ((x_hbm, xbuf, width), (w_hbm, wbuf, N), (r_hbm, rbuf, N))
    order = (1, 2, 0)

    def kinds_of(u):
        return order if u % PARTS == 0 else (0,)

    def slot(k, u):
        return u if k == 0 else u // PARTS

    def source(k, u, owner, start, rows):
        ref, _, wide = kinds[k]
        place = owner * units + u if k == 0 else owner * groups + u // PARTS
        at = pl.multiple_of(place * wide, wide)
        return ref.at[pl.ds(start, rows), pl.ds(at, wide)]

    def landing(k, u, rows):
        return kinds[k][1].at[slot(k, u), rows]

    def rows_of(owner, edge):
        start = EDGE + owner * tl + edge * (tl - EDGE)
        return pl.ds(pl.multiple_of(start, 8), EDGE if edge else tl - EDGE)

    def taken(k, u, owner, edge):
        return source(k, u, owner, edge * (tl - EDGE), EDGE if edge else tl - EDGE)

    def own_copy(k, u, edge):
        return pltpu.make_async_copy(
            taken(k, u, h, edge), landing(k, u, rows_of(h, edge)), yrec.at[u, 0, k + 3 * edge]
        )

    def head_copy(k, u, d, sender, edge):
        return pltpu.make_async_remote_copy(
            src_ref=taken(k, u, (h + d) % nh, edge),
            dst_ref=landing(k, u, rows_of(sender, edge)),
            send_sem=ysem.at[u, d, k + 3 * edge],
            recv_sem=yrec.at[u, d, k + 3 * edge],
            device_id=(c, (h + d) % nh),
            device_id_type=MESH,
        )

    def decay_rows(owner):
        return lbuf.at[pl.ds(pl.multiple_of(owner * tl, 8), tl)]

    def decay_own():
        return pltpu.make_async_copy(l_hbm, decay_rows(h), lrec.at[0])

    def decay_copy(d, sender):
        return pltpu.make_async_remote_copy(
            src_ref=l_hbm,
            dst_ref=decay_rows(sender),
            send_sem=lsem.at[d],
            recv_sem=lrec.at[d],
            device_id=(c, (h + d) % nh),
            device_id_type=MESH,
        )

    def edge_copy(k, u):
        return pltpu.make_async_remote_copy(
            src_ref=landing(k, u, pl.ds(tokens, EDGE)),
            dst_ref=landing(k, u, pl.ds(0, EDGE)),
            send_sem=hsem.at[u, k],
            recv_sem=hrec.at[u, k],
            device_id=(lax.rem(c + 1, nc), h),
            device_id_type=MESH,
        )

    decay_own().start()
    for d in range(1, nh):
        decay_copy(d, h).start()
    for edge in (1, 0):
        for u in range(units):
            for k in kinds_of(u):
                own_copy(k, u, edge).start()
                for d in range(1, nh):
                    head_copy(k, u, d, h, edge).start()

    @pl.when(c == 0)
    def _():
        for g in range(units):
            for k in kinds_of(g):
                wide = kinds[k][2]
                kinds[k][1][slot(k, g), 0:EDGE, :] = jnp.zeros((EDGE, wide), f32)

    decay_own().wait()
    for d in range(1, nh):
        decay_copy(d, (h - d + nh) % nh).wait_recv()
    target = lax.broadcasted_iota(jnp.int32, (tokens, tokens), 0)
    origin = lax.broadcasted_iota(jnp.int32, (tokens, tokens), 1)
    past = target >= origin
    near = jnp.logical_and(past, target // CHUNK == origin // CHUNK)
    decay3 = split3(lbuf[...])
    for which, mask in ((0, near), (1, past)):
        ones = jnp.where(mask, 1.0, 0.0).astype(bf16)
        total = dot(ones, decay3[0]) + dot(ones, decay3[1]) + dot(ones, decay3[2])
        for part, piece in enumerate(split3(total)):
            cums[which, part] = piece

    last = (h + 1) % nh
    for u in range(units):
        for k in kinds_of(u):

            @pl.when(h == nh - 1)
            def _():
                own_copy(k, u, 1).wait()

            @pl.when(h < nh - 1)
            def _():
                head_copy(k, u, last, nh - 1, 1).wait_recv()

            @pl.when(gives_edge)
            def _():
                edge_copy(k, u).start()

    def spread(which, g, lane):
        head_at = lax.broadcasted_iota(jnp.int32, (H, LANES), 0)
        channel = lax.broadcasted_iota(jnp.int32, (H, LANES), 1)
        wanted = h * heads_here + g * per_unit + (lane + channel) // P_SIZE
        ones = jnp.where(head_at == wanted, 1.0, 0.0).astype(bf16)
        return (
            dot(cums[which, 0], ones) + dot(cums[which, 1], ones) + dot(cums[which, 2], ones)
        )

    def peer_copy(src, dst, send, recv, ctx):
        return pltpu.make_async_remote_copy(
            src_ref=src,
            dst_ref=dst,
            send_sem=send,
            recv_sem=recv,
            device_id=(ctx, h),
            device_id_type=MESH,
        )

    piece_rows = sbuf.shape[2] // PIECES

    def rows_at(i):
        return pl.ds(i * piece_rows, piece_rows)

    def core_copy(g):
        return peer_copy(sbuf.at[g, 1 - core], arecv.at[g], asem.at[g], arec.at[g], core_peer)

    def side_copy(g, i):
        return peer_copy(
            bsend.at[g, rows_at(i)], brecv.at[g, rows_at(i)], bsem.at[g, i], brec.at[g, i], side_peer
        )

    def plane_copy(g, i):
        return peer_copy(
            csend.at[g, rows_at(i)],
            crecv.at[g, rows_at(i)],
            csem.at[g, i],
            crec.at[g, i],
            lax.rem(c + 4, nc),
        )

    def back_copy(g, i):
        return peer_copy(
            dsend.at[g, rows_at(i)],
            inbuf.at[g, core, rows_at(i)],
            dsem.at[g, i],
            drec.at[g, i],
            core_peer,
        )

    def back_arrival(g, i):
        return peer_copy(
            dsend.at[g, rows_at(i)],
            inbuf.at[g, 1 - core, rows_at(i)],
            dsem.at[g, i],
            drec.at[g, i],
            core_peer,
        )

    def arrive(k, u):
        own_copy(k, u, 0).wait()

        @pl.when(c > 0)
        def _():
            edge_copy(k, u).wait_recv()

        @pl.when(h < nh - 1)
        def _():
            own_copy(k, u, 1).wait()

        for d in range(1, nh):
            head_copy(k, u, d, (h - d + nh) % nh, 0).wait_recv()

            @pl.when(d != last)
            def _():
                head_copy(k, u, d, (h - d + nh) % nh, 1).wait_recv()

    def project(u):
        g = u // PARTS
        for k in (1, 2):
            arrive(k, u)
        at = pl.multiple_of((h * groups + g) * N, N)
        writes = conv(wbuf[g], cw_ref[:, pl.ds(at, N)], tokens)
        reads = conv(rbuf[g], cr_ref[:, pl.ds(at, N)], tokens)
        reads2 = split2(reads)
        writes2 = split2(writes)
        creads[g, 0] = reads2[0]
        creads[g, 1] = reads2[1]
        row = lax.broadcasted_iota(jnp.int32, (CHUNK, CHUNK), 0)
        column = lax.broadcasted_iota(jnp.int32, (CHUNK, CHUNK), 1)
        for k in range(tokens // CHUNK):
            part = slice(k * CHUNK, (k + 1) * CHUNK)
            scores = dot3(
                (reads2[0][part], reads2[1][part]),
                (writes2[0][part], writes2[1][part]),
                ((1,), (1,)),
            )
            scores = split2(jnp.where(row >= column, scores, 0.0))
            gm[k, 0] = scores[0]
            gm[k, 1] = scores[1]
            turned = split2(jnp.transpose(writes[part]))
            bt[k, 0] = turned[0]
            bt[k, 1] = turned[1]

    def local(u):
        @pl.when(u % PARTS == 0)
        def _():
            project(u)

        g = u // PARTS
        arrive(0, u)

        def lanes(b, carry):
            lane = pl.multiple_of(b * LANES, LANES)
            cols = pl.ds(lane, LANES)
            taps = cf_ref[:, pl.ds(pl.multiple_of((h * units + u) * width + lane, LANES), LANES)]
            spaced = spread(0, u, lane)
            state = None
            for k in range(tokens // CHUNK):
                part = slice(k * CHUNK, (k + 1) * CHUNK)
                act = conv(xbuf[u, k * CHUNK : k * CHUNK + CHUNK + EDGE, cols], taps, CHUNK)
                log = spaced[part]
                scaled = split2(act * jnp.exp(-log))
                mixed = dot3((gm[k, 0], gm[k, 1]), scaled)
                added = dot3((bt[k, 0], bt[k, 1]), scaled)
                if k > 0:
                    mixed = mixed + dot3((creads[g, 0, part], creads[g, 1, part]), split2(state))
                    added = added + state
                yloc[u, part, cols] = mixed * jnp.exp(log)
                state = added * jnp.exp(log[CHUNK - 1 : CHUNK])
            ends = spread(1, u, lane)[tokens - 1 : tokens]
            fade = jnp.broadcast_to(jnp.exp(ends), (EDGE, LANES))
            for half in range(2):
                sbuf[u, half, 0:EDGE, cols] = fade
                sbuf[u, half, EDGE : EDGE + N // 2, cols] = state[half * N // 2 : (half + 1) * N // 2]
            return carry

        lax.fori_loop(0, width // LANES, lanes, 0)
        core_copy(u).start()

    def pair(g):
        core_copy(g).wait_recv()
        mine_first = core == 0
        mine_fade = sbuf[g, core, 0:1]
        peer_fade = arecv[g, 0:1]
        late_fade = jnp.where(mine_first, peer_fade, mine_fade)
        for i in range(PIECES):
            rows = slice(i * piece_rows, (i + 1) * piece_rows)
            mine = sbuf[g, core, rows]
            peer = arecv[g, rows]
            first = jnp.where(mine_first, mine, peer)
            late = jnp.where(mine_first, peer, mine)
            bsend[g, rows] = late_fade * first + late
            if i == 0:
                bsend[g, 0:EDGE] = jnp.broadcast_to(mine_fade * peer_fade, (EDGE, width))
            side_copy(g, i).start()

    def chain(g):
        side_first = side == 0
        for i in range(PIECES):
            rows = slice(i * piece_rows, (i + 1) * piece_rows)
            side_copy(g, i).wait_recv()

            @pl.when(plane == 0)
            def _():
                crecv[g, rows] = jnp.zeros((piece_rows, width), f32)

            @pl.when(plane > 0)
            def _():
                plane_copy(g, i).wait_recv()

            @pl.when(plane < planes - 1)
            def _():
                mine_fade = bsend[g, 0:1]
                peer_fade = brecv[g, 0:1]
                mine = bsend[g, rows]
                peer = brecv[g, rows]
                first = jnp.where(side_first, mine, peer)
                late = jnp.where(side_first, peer, mine)
                late_fade = jnp.where(side_first, peer_fade, mine_fade)
                csend[g, rows] = (mine_fade * peer_fade) * crecv[g, rows] + (
                    late_fade * first + late
                )
                plane_copy(g, i).start()

        mine_fade = bsend[g, 0:1]
        peer_fade = brecv[g, 0:1]
        first_fade = jnp.where(side_first, mine_fade, peer_fade)
        lead_fade = jnp.where(core == 0, sbuf[g, core, 0:1], arecv[g, 0:1])
        for i in range(PIECES):
            rows = slice(i * piece_rows, (i + 1) * piece_rows)
            first = jnp.where(side_first, bsend[g, rows], brecv[g, rows])
            entering = crecv[g, rows]
            even = jnp.where(side_first, entering, first_fade * entering + first)
            lead = jnp.where(core == 0, sbuf[g, core, rows], arecv[g, rows])
            odd = lead_fade * even + lead
            inbuf[g, core, rows] = jnp.where(core == 0, even, odd)
            dsend[g, rows] = jnp.where(core == 0, odd, even)
            back_copy(g, i).start()

    def finish(u):
        g = u // PARTS
        for i in range(PIECES):
            back_arrival(u, i).wait_recv()

        def lanes(b, squares):
            lane = pl.multiple_of(b * LANES, LANES)
            cols = pl.ds(lane, LANES)
            state = jnp.concatenate(
                [
                    inbuf[u, 0, EDGE : EDGE + N // 2, cols],
                    inbuf[u, 1, EDGE : EDGE + N // 2, cols],
                ],
                0,
            )
            carried = dot3((creads[g, 0], creads[g, 1]), split2(state))
            mixed = yloc[u, :, cols] + carried * jnp.exp(spread(1, u, lane))
            yloc[u, :, cols] = mixed
            squared = mixed * mixed
            for at in range(0, LANES, 128):
                squares = squares + squared[:, at : at + 128]
            return squares

        before = jnp.where(u % PARTS == 0, 0.0, 1.0) * squares_ref[...]
        squares_ref[...] = lax.fori_loop(0, width // LANES, lanes, before)

        @pl.when(u % PARTS == PARTS - 1)
        def _():
            mean = jnp.sum(squares_ref[...], 1, keepdims=True) / (width * PARTS)
            inverse = lax.rsqrt(mean + eps_norm)
            for back in range(PARTS - 1, -1, -1):
                cols = pl.ds(pl.multiple_of((u - back) * width, width), width)
                out_ref[:, cols] = yloc[u - back] * inverse

    def step(i, carry):
        @pl.when(i < units)
        def _():
            local(i)
            pair(i)

        @pl.when(jnp.logical_and(i >= 1, i < units + 1))
        def _():
            chain(i - 1)

        @pl.when(i >= 2)
        def _():
            finish(i - 2)

        return carry

    squares_ref[...] = jnp.zeros((tokens, 128), f32)
    lax.fori_loop(0, units + 2, step, 0)

    for d in range(1, nh):
        decay_copy(d, h).wait_send()
    for g in range(units):
        core_copy(g).wait_send()
        for d in range(1, nh):
            for k in kinds_of(g):
                head_copy(k, g, d, h, 0).wait_send()
                head_copy(k, g, d, h, 1).wait_send()

        @pl.when(gives_edge)
        def _():
            for k in kinds_of(g):
                edge_copy(k, g).wait_send()

        for i in range(PIECES):
            side_copy(g, i).wait_send()
            back_copy(g, i).wait_send()

            @pl.when(plane < planes - 1)
            def _():
                plane_copy(g, i).wait_send()


def shards(
    features, state_write, state_read, log_decay, conv_features, conv_write, conv_read, norm_gain
):
    nh = lax.axis_size("head")
    nc = lax.axis_size("ctx")
    groups = G // nh
    units = groups * PARTS
    tokens = features.shape[0] * nh
    width = features.shape[1] // (G * PARTS)
    half = N // 2 + EDGE
    count = tokens // CHUNK
    vm = pltpu.VMEM
    dma = pltpu.SemaphoreType.DMA
    anywhere = pl.BlockSpec(memory_space=pl.ANY)
    near = pl.BlockSpec(memory_space=pltpu.VMEM)
    mixed = pl.pallas_call(
        functools.partial(kernel, nh, nc),
        out_shape=pltpu.VMEM((tokens, units * width), f32),
        in_specs=[anywhere] * 4 + [near] * 3,
        out_specs=near,
        scratch_shapes=[
            vm((units, EDGE + tokens, width), f32),
            vm((groups, EDGE + tokens, N), f32),
            vm((groups, EDGE + tokens, N), f32),
            vm((tokens, H), f32),
            vm((units, tokens, width), f32),
            vm((2, 3, tokens, H), bf16),
            vm((tokens, 128), f32),
            vm((groups, 2, tokens, N), bf16),
            vm((count, 2, CHUNK, CHUNK), bf16),
            vm((count, 2, N, CHUNK), bf16),
            vm((units, 2, half, width), f32),
            vm((units, half, width), f32),
            vm((units, half, width), f32),
            vm((units, half, width), f32),
            vm((units, half, width), f32),
            vm((units, half, width), f32),
            vm((units, half, width), f32),
            vm((units, 2, half, width), f32),
            dma((units, nh, 6)),
            dma((units, nh, 6)),
            dma((nh,)),
            dma((nh,)),
            dma((units, 3)),
            dma((units, 3)),
            dma((units,)),
            dma((units,)),
            dma((units, PIECES)),
            dma((units, PIECES)),
            dma((units, PIECES)),
            dma((units, PIECES)),
            dma((units, PIECES)),
            dma((units, PIECES)),
        ],
        compiler_params=pltpu.CompilerParams(
            collective_id=0, has_side_effects=True, vmem_limit_bytes=58 * 1024 * 1024
        ),
    )(features, state_write, state_read, log_decay, conv_features, conv_write, conv_read)
    return mixed * norm_gain


def solution(mesh):
    return jax.shard_map(
        shards,
        mesh=mesh,
        in_specs=(
            P(("ctx", "head"), None),
            P(("ctx", "head"), None),
            P(("ctx", "head"), None),
            P(("ctx", "head"), None),
            P(),
            P(),
            P(),
            P("head"),
        ),
        out_specs=P("ctx", "head"),
        check_vma=False,
    )
```
